32 devices in a mesh: gx: 2 (over y), gy: 4 (over x, core), gz: 4 (over z).
Axes of the slice: x: 2, y: 2, z: 4, core: 2. Of those that a mesh axis runs over, the one named last changes fastest.
Arguments:
- coeffs: bfloat16 [2, 4, 4, 128, 3200], P('gx', 'gy', 'gz'), may hold values from -6 to 6
- halo_rows: int32 [2, 4, 4, 32], P('gx', 'gy', 'gz'), may hold values from 0 to 127
- edge_source: int32 [2, 4, 4, 4, 128], P('gx', 'gy', 'gz'), may hold values from 0 to 991
- edge_target: int32 [2, 4, 4, 4, 128], P('gx', 'gy', 'gz'), may hold values from 0 to 127
- edge_count: int32 [2, 4, 4, 4], P('gx', 'gy', 'gz'), may hold values from 1 to 128
- block_count: int32 [2, 4, 4], P('gx', 'gy', 'gz'), may hold values from 0 to 4, as said below
- wigner: bfloat16 [2, 4, 4, 4, 165, 128], P('gx', 'gy', 'gz'), may hold values from -2.6875 to 2.6875
- w_zero: bfloat16 [2, 640, 640], replicated, may hold values from -0.25 to 0.25
- w_one: bfloat16 [2, 2, 512, 512], replicated, may hold values from -0.1875 to 0.1875
- w_two: bfloat16 [2, 2, 384, 384], replicated, may hold values from -0.21875 to 0.21875
- attn_vector: float32 [128], replicated, may hold values from -3 to 3
Outputs:
- update: bfloat16 [2, 4, 4, 128, 3200], P('gx', 'gy', 'gz')
The draws below stay inside these ranges and needn't reach their ends.
Inputs may be any that keep to these rules, and one draw needn't show every extreme that they name: `edge_source`: rows of the home device's source table: 128 own atoms, then 27 blocks of 32. Devices 2i and 2i + 1 along gz (same gx and gy) hold 4 live blocks together; the live blocks of a home are its first block_count ones.
All inputs are finite; a program needn't handle non-finite values.
Results may differ from the reference program's by a relative error of at most 0.0079.
Values may be sent and summed in bfloat16 or wider, within the bound.
No kernel may reach another device: no remote copies, remote signals or barrier semaphores. Data moves between devices by JAX's collectives and lax.ppermute only.
A program may use at most 128 MiB of HBM per device.

```python
import math
import jax
import jax.numpy as jnp
import numpy as np
from jax import lax

CH = 128
HEADS = 8
A_DEV = 128
BLOCK = 128
SLOTS = 2
HOMEB = 4
HB = 32
POOL = 992
N_GX = 2
N_GY = 4
N_GZ = 4


def draw_block_count(key, part):
    pairs = N_GX * N_GY * (N_GZ // 2)
    moved = jax.random.randint(jax.random.fold_in(key, 11), (pairs,), -SLOTS, SLOTS + 1)
    forced = jax.random.randint(jax.random.fold_in(key, 12), (), 0, pairs)
    direction = 2 * jax.random.randint(jax.random.fold_in(key, 13), (), 0, 2) - 1
    moved = jnp.where(jnp.arange(pairs) == forced, SLOTS * direction, moved)
    lower = SLOTS + moved
    upper = SLOTS - moved
    stacked = jnp.stack([lower, upper], axis=-1).reshape(N_GX, N_GY, N_GZ)
    return stacked.astype(jnp.int32)


def plant(drawn, stream_key, low, top_value):
    dims = drawn.shape
    spot = [jax.random.randint(jax.random.fold_in(stream_key, axis), (), 0, dims[axis]) for axis in range(len(dims))]
    drawn = drawn.at[tuple(spot)].set(low)
    longest = dims.index(max(dims))
    spot[longest] = (spot[longest] + 1) % dims[longest]
    return drawn.at[tuple(spot)].set(top_value)


def levels(stream_key, shape, cuts, least, top_value):
    level, own = 1.0, jax.random.fold_in(stream_key, 6)
    for axis_at, blocks in cuts:
        heights = jnp.exp(jax.random.uniform(jax.random.fold_in(own, axis_at), (blocks,), jnp.float32, least / len(cuts), top_value / len(cuts)))
        level = level * jnp.repeat(heights, shape[axis_at] // blocks).reshape([-1 if axis == axis_at else 1 for axis in range(len(shape))])
    return level


def noise(key, dims, spread, limit, cuts=(), kind=jnp.bfloat16):
    level = levels(key, dims, cuts, -0.22, 0.18) if cuts else 1.0
    drawn = jax.random.normal(key, dims, jnp.float32) * spread * level
    return jnp.minimum(jnp.maximum(drawn, -limit), limit).astype(kind)


def setup_inputs(seed: int = 0) -> dict:
    streams_of = jax.random.split(jax.random.key(seed), 12)
    coeffs = noise(streams_of[0], (N_GX, N_GY, N_GZ, A_DEV, 25 * CH), 1.0, 6.0, ((0, 2), (1, 4), (2, 4)))
    halo_rows = plant(jax.random.randint(streams_of[1], (N_GX, N_GY, N_GZ, HB), 0, A_DEV), jax.random.fold_in(streams_of[1], 1), 0, A_DEV - 1).astype(jnp.int32)
    edge_source = plant(jax.random.randint(streams_of[2], (N_GX, N_GY, N_GZ, HOMEB, BLOCK), 0, POOL), jax.random.fold_in(streams_of[2], 1), 0, POOL - 1).astype(jnp.int32)
    edge_target = plant(jax.random.randint(streams_of[3], (N_GX, N_GY, N_GZ, HOMEB, BLOCK), 0, A_DEV), jax.random.fold_in(streams_of[3], 1), 0, A_DEV - 1).astype(jnp.int32)
    edge_count = plant(jax.random.randint(streams_of[4], (N_GX, N_GY, N_GZ, HOMEB), 1, BLOCK + 1), jax.random.fold_in(streams_of[4], 1), 1, BLOCK).astype(jnp.int32)
    block_count = draw_block_count(jax.random.fold_in(streams_of[11], 71), 0)
    wigner = noise(streams_of[6], (N_GX, N_GY, N_GZ, HOMEB, 165, BLOCK), 0.45, 2.6875, ((0, 2), (1, 4), (2, 4)))
    w_zero = noise(streams_of[7], (2, 5 * CH, 5 * CH), (5 * CH) ** -0.5, 0.25)
    w_one = noise(streams_of[8], (2, 2, 4 * CH, 4 * CH), (8 * CH) ** -0.5, 0.1875)
    w_two = noise(streams_of[9], (2, 2, 3 * CH, 3 * CH), (6 * CH) ** -0.5, 0.21875)
    attn_vector = noise(streams_of[10], (CH,), 0.5, 3.0, (), jnp.float32)
    return dict(coeffs=coeffs, halo_rows=halo_rows, edge_source=edge_source, edge_target=edge_target, edge_count=edge_count, block_count=block_count, wigner=wigner, w_zero=w_zero, w_one=w_one, w_two=w_two, attn_vector=attn_vector)


EPS = 1e-06

def keep_index():
    ordering = [0, 2, 6, 12, 20, 3, 7, 13, 21, 1, 5, 11, 19, 8, 14, 22, 4, 10, 18]
    starts = [0, 1, 10, 35, 84]
    lookup = np.full((19, 25), 165, dtype=np.int32)
    for row_pos, component in enumerate(ordering):
        degree = math.isqrt(component)
        offset = component - degree * degree
        for column in range(2 * degree + 1):
            lookup[row_pos, degree * degree + column] = starts[degree] + offset * (2 * degree + 1) + column
    return lookup

def expand_frames(packed):
    padded = jnp.concatenate([packed, jnp.zeros_like(packed[:, :1])], axis=1)
    picked = jnp.take(padded, jnp.asarray(keep_index().reshape(-1)), axis=1)
    return picked.reshape(packed.shape[0], 19, 25, packed.shape[2])

def rms_norm(values):
    widened = values.astype(jnp.float32)
    factor = lax.rsqrt(lax.optimization_barrier(jnp.mean(widened * widened, axis=-1, keepdims=True)) + EPS)
    return (widened * factor).astype(jnp.bfloat16)

def product(left, right):
    return jnp.dot(left, right, preferred_element_type=jnp.float32)

def degree_mix(inputs, weight_zero, weight_one, weight_two):
    zero_out = product(inputs[:, :5 * CH], weight_zero)
    plus_one = inputs[:, 5 * CH:9 * CH]
    minus_one = inputs[:, 9 * CH:13 * CH]
    plus_two = inputs[:, 13 * CH:16 * CH]
    minus_two = inputs[:, 16 * CH:]
    one_plus = product(plus_one, weight_one[0]) - product(minus_one, weight_one[1])
    one_minus = product(minus_one, weight_one[0]) + product(plus_one, weight_one[1])
    two_plus = product(plus_two, weight_two[0]) - product(minus_two, weight_two[1])
    two_minus = product(minus_two, weight_two[0]) + product(plus_two, weight_two[1])
    return jnp.concatenate([zero_out, one_plus, one_minus, two_plus, two_minus], axis=1)

def edge_work(rotated, live_mask, w_zero, w_one, w_two, attn_vector):
    edge_total = rotated.shape[0]
    mixed_one = degree_mix(rotated, w_zero[0], w_one[0], w_two[0])
    scalars = mixed_one[:, :CH]
    logits = lax.optimization_barrier(jnp.sum((jax.nn.silu(scalars) * attn_vector).reshape(edge_total, HEADS, CH // HEADS), axis=-1))
    weights = jax.nn.sigmoid(logits) * live_mask[:, None]
    higher = mixed_one[:, CH:].reshape(edge_total, 18, CH) * jax.nn.sigmoid(scalars)[:, None, :]
    activated = jnp.concatenate([jax.nn.silu(scalars), higher.reshape(edge_total, 18 * CH)], axis=1).astype(jnp.bfloat16)
    mixed_two = degree_mix(activated, w_zero[1], w_one[1], w_two[1])
    weighted = mixed_two.reshape(edge_total, 19, HEADS, CH // HEADS) * weights[:, None, :, None]
    return weighted.reshape(edge_total, 19 * CH).astype(jnp.bfloat16)

def reference(coeffs, halo_rows, edge_source, edge_target, edge_count, block_count, wigner, w_zero, w_one, w_two, attn_vector):
    feature_width = 25 * CH
    normed = rms_norm(coeffs)
    boundary = jnp.take_along_axis(normed, halo_rows[..., None], axis=3)

    def device(flat_id):
        grid_x = flat_id // (N_GY * N_GZ)
        grid_y = flat_id // N_GZ % N_GY
        grid_z = flat_id % N_GZ
        pieces = [normed[grid_x, grid_y, grid_z]]
        for step_x in (-1, 0, 1):
            for step_y in (-1, 0, 1):
                for step_z in (-1, 0, 1):
                    pieces.append(boundary[(grid_x + step_x) % N_GX, (grid_y + step_y) % N_GY, (grid_z + step_z) % N_GZ])
        source_table = jnp.concatenate(pieces, axis=0)
        sources = edge_source[grid_x, grid_y, grid_z]
        targets = edge_target[grid_x, grid_y, grid_z]
        counts = edge_count[grid_x, grid_y, grid_z]
        owned = block_count[grid_x, grid_y, grid_z]
        frames = expand_frames(wigner[grid_x, grid_y, grid_z]).astype(jnp.float32)
        gathered = source_table[sources.reshape(-1)].reshape(HOMEB, BLOCK, 25, CH).astype(jnp.float32)
        rotated = jnp.einsum('gije,gejc->geic', frames, gathered).astype(jnp.bfloat16)
        edge_pos = jnp.arange(BLOCK, dtype=jnp.int32)[None, :]
        block_pos = jnp.arange(HOMEB, dtype=jnp.int32)[:, None]
        live_mask = ((edge_pos < counts[:, None]) & (block_pos < owned)).astype(jnp.float32).reshape(-1)
        weighted = edge_work(rotated.reshape(HOMEB * BLOCK, 19 * CH), live_mask, w_zero, w_one, w_two, attn_vector)
        weighted = weighted.reshape(HOMEB, BLOCK, 19, CH).astype(jnp.float32)
        message = jnp.einsum('gije,geic->gejc', frames, weighted).astype(jnp.bfloat16)
        summed = jnp.zeros((A_DEV, feature_width), jnp.float32)
        summed = summed.at[targets.reshape(-1)].add(message.reshape(HOMEB * BLOCK, feature_width).astype(jnp.float32))
        return summed.astype(jnp.bfloat16)
    result = lax.map(device, jnp.arange(N_GX * N_GY * N_GZ, dtype=jnp.int32))
    return result.reshape(N_GX, N_GY, N_GZ, A_DEV, feature_width)
```

```python
import functools
import math

import jax
import jax.numpy as jnp
from jax import lax
from jax.experimental import pallas as pl
from jax.experimental.pallas import tpu as pltpu
from jax.sharding import PartitionSpec as P

CH = 128
HEADS = 8
ORDER = (0, 2, 6, 12, 20, 3, 7, 13, 21, 1, 5, 11, 19, 8, 14, 22, 4, 10, 18)
KEPT = len(ORDER)
COMPS = 25
STARTS = (0, 1, 10, 35, 84)
PACKED = 165
EPS = 1e-06
TILE = 256
VMEM = pltpu.VMEM
F32 = jnp.float32
BF16 = jnp.bfloat16


def rows_of_degree(degree):
    found = []
    for place, component in enumerate(ORDER):
        if math.isqrt(component) == degree:
            found.append((place, component - degree * degree))
    return found


def weight_row(degree, offset, column):
    return STARTS[degree] + offset * (2 * degree + 1) + column


def full(shape):
    return pl.BlockSpec(shape, lambda: (0,) * len(shape))


def boundary_kernel(halo_ref, coeffs_ref, out_ref):
    atoms = coeffs_ref.shape[0]
    count = halo_ref.shape[1]
    picked = (
        lax.broadcasted_iota(jnp.int32, (atoms, count), 0) == halo_ref[...]
    ).astype(F32).T.astype(BF16)
    rows = jnp.dot(picked, coeffs_ref[...], preferred_element_type=F32)
    mean = jnp.mean(rows * rows, axis=-1, keepdims=True)
    out_ref[...] = (rows * lax.rsqrt(mean + EPS)).astype(BF16)


def boundary_rows(coeffs, halo):
    return pl.pallas_call(
        boundary_kernel,
        out_shape=jax.ShapeDtypeStruct((halo.shape[1], coeffs.shape[1]), BF16),
        name="boundary",
    )(halo, coeffs)


def prep_kernel(
    luts, scalar_ref, count_ref, source_ref, target_ref, wigner_ref, coeffs_ref,
    normed_ref, *out_refs,
):
    atoms, rows_each, passes, lut_even, lut_odd, pass_even, pass_odd = luts
    values = coeffs_ref[...].astype(F32)
    mean = jnp.mean(values * values, axis=-1, keepdims=True)
    normed_ref[...] = (values * lax.rsqrt(mean + EPS)).astype(BF16)

    blocks, size = source_ref.shape
    owned = scalar_ref[0]
    odd = scalar_ref[1] == 1
    source = source_ref[...]
    target = target_ref[...]
    row = source
    stage = jnp.zeros_like(source)
    for place in range(len(lut_even)):
        low = atoms + rows_each * place
        base = jnp.where(odd, lut_odd[place], lut_even[place])
        which = jnp.where(odd, pass_odd[place], pass_even[place])
        inside = source >= low
        row = jnp.where(inside, source - low + base, row)
        stage = jnp.where(inside, which, stage)
    lane = lax.broadcasted_iota(jnp.int32, (blocks, size), 1)
    block = lax.broadcasted_iota(jnp.int32, (blocks, size), 0)
    limit = jnp.zeros_like(source)
    for g in range(blocks):
        limit = jnp.where(block == g, count_ref[g], limit)
    live = (lane < limit) & (block < owned)
    high = row // 128
    low_part = row - high * 128

    at_row = lax.broadcasted_iota(jnp.int32, (size, size), 0)
    at_col = lax.broadcasted_iota(jnp.int32, (size, size), 1)
    upper = (at_row < at_col).astype(BF16)
    diagonal = at_row == at_col
    slots = blocks * size
    slot = lax.broadcasted_iota(jnp.int32, (size, slots), 1)
    for index in range(passes):
        packed_ref, aux_ref, total_ref = out_refs[3 * index : 3 * index + 3]
        mine = live & (stage == index)
        ones = mine.astype(F32)
        before = jnp.dot(ones.astype(BF16), upper, preferred_element_type=F32)
        packed = jnp.zeros((PACKED, slots), F32)
        aux = jnp.zeros((8, slots), F32)
        start = jnp.zeros((1, 1), F32)
        for g in range(blocks):
            rank = jnp.where(mine[g : g + 1], before[g : g + 1] + start, -1.0)
            column = jnp.sum(
                jnp.where(diagonal, jnp.broadcast_to(rank, (size, size)), 0.0),
                axis=1, keepdims=True,
            ).astype(jnp.int32)
            place = (column == slot).astype(BF16)
            packed += jnp.dot(wigner_ref[g], place, preferred_element_type=F32)
            extra = jnp.concatenate(
                [high[g : g + 1], low_part[g : g + 1], target[g : g + 1],
                 jnp.zeros((5, size), jnp.int32)], axis=0,
            ).astype(F32).astype(BF16)
            aux += jnp.dot(extra, place, preferred_element_type=F32)
            start = start + jnp.sum(ones[g : g + 1], axis=1, keepdims=True)
        packed_ref[...] = packed
        aux_ref[...] = jnp.concatenate(
            [aux[0:1] * 128.0 + aux[1:2], aux[2:3], aux[2:8]], axis=0
        )
        total_ref[0] = jnp.sum(ones).astype(jnp.int32)


def prepare(luts, scalars, counts, source, target, wigner, coeffs):
    passes = luts[2]
    slots = source.shape[0] * source.shape[1]
    smem = pl.BlockSpec(memory_space=pltpu.SMEM)
    vmem = pl.BlockSpec(memory_space=VMEM)
    shapes = [jax.ShapeDtypeStruct(coeffs.shape, BF16)]
    specs = [vmem]
    for _ in range(passes):
        shapes += [
            jax.ShapeDtypeStruct((PACKED, slots), F32),
            jax.ShapeDtypeStruct((8, slots), F32),
            jax.ShapeDtypeStruct((1,), jnp.int32),
        ]
        specs += [vmem, vmem, smem]
    return pl.pallas_call(
        functools.partial(prep_kernel, luts),
        out_shape=shapes,
        in_specs=[smem, smem, vmem, vmem, vmem, vmem],
        out_specs=specs,
        name="prepare",
    )(scalars, counts, source, target, wigner, coeffs)


def edge_kernel(sizes, has_acc, last, *refs):
    n_tab = len(sizes)
    total_ref, packed_ref, aux_ref, attn_ref = refs[:4]
    tab_refs = refs[4 : 4 + n_tab]
    w_refs = refs[4 + n_tab : 7 + n_tab]
    at = 7 + n_tab
    acc_in = None
    if has_acc:
        acc_in = refs[at]
        at += 1
    out_ref = refs[at]
    (table, table_t, grid, rot, hid, msg, acc, w0, w1, w2, tab_sem, w_sem) = refs[at + 1 :]

    copies = []
    start = 0
    for index, ref in enumerate(tab_refs):
        copy = pltpu.make_async_copy(
            ref, table.at[pl.ds(start, sizes[index]), :], tab_sem.at[index]
        )
        copy.start()
        copies.append(copy)
        start += sizes[index]
    w_copies = []
    for index, (ref, dst) in enumerate(zip(w_refs, (w0, w1, w2))):
        copy = pltpu.make_async_copy(ref, dst, w_sem.at[index])
        copy.start()
        w_copies.append(copy)
    if has_acc:
        acc_copy = pltpu.make_async_copy(acc_in, acc, w_sem.at[3])
        acc_copy.start()
    padded = table.shape[0]
    if start < padded:
        table[pl.ds(start, padded - start), :] = jnp.zeros(
            (padded - start, table.shape[1]), BF16
        )
    for copy in copies:
        copy.wait()

    @pl.loop(0, COMPS)
    def _(j):
        at_j = pl.multiple_of(j * CH, CH)
        table_t[pl.ds(at_j, CH), :] = table[:, pl.ds(at_j, CH)].T

    for copy in w_copies:
        copy.wait()
    if has_acc:
        acc_copy.wait()
    else:
        acc[...] = jnp.zeros_like(acc)

    def tile(t, carry):
        lanes = pl.ds(pl.multiple_of(t * TILE, TILE), TILE)
        source = aux_ref[0:1, lanes].astype(jnp.int32)
        target = aux_ref[1:2, lanes].astype(jnp.int32)
        onehot = (
            lax.broadcasted_iota(jnp.int32, (padded, TILE), 0) == source
        ).astype(BF16)

        @pl.loop(0, 5)
        def _(part):
            part_rows = pl.ds(pl.multiple_of(part * 5 * CH, 5 * CH), 5 * CH)
            grid[part_rows, :] = jnp.dot(
                table_t[part_rows, :], onehot, preferred_element_type=F32
            )

        @pl.loop(0, CH // 16)
        def _(c):
            base = c * 16
            for degree in range(5):
                width = 2 * degree + 1
                inputs = [
                    grid[pl.ds(pl.multiple_of((degree * degree + j) * CH + base, 16), 16), :]
                    for j in range(width)
                ]
                for place, offset in rows_of_degree(degree):
                    total = None
                    for j in range(width):
                        k = weight_row(degree, offset, j)
                        term = packed_ref[k : k + 1, lanes] * inputs[j]
                        total = term if total is None else total + term
                    rot[pl.ds(pl.multiple_of(place * CH + base, 16), 16), :] = total.astype(BF16)

        def conv(index):
            hid[0 : 5 * CH, :] = jnp.dot(
                w0[index], rot[0 : 5 * CH, :], preferred_element_type=F32
            )
            for low, width, w in ((5 * CH, 4 * CH, w1), (13 * CH, 3 * CH, w2)):
                plus = rot[low : low + width, :]
                minus = rot[low + width : low + 2 * width, :]
                hid[low : low + width, :] = jnp.dot(
                    w[index, 0], plus, preferred_element_type=F32
                ) - jnp.dot(w[index, 1], minus, preferred_element_type=F32)
                hid[low + width : low + 2 * width, :] = jnp.dot(
                    w[index, 0], minus, preferred_element_type=F32
                ) + jnp.dot(w[index, 1], plus, preferred_element_type=F32)

        conv(0)
        scalars = hid[0:CH, :]
        gate = jax.nn.sigmoid(scalars)
        silu = scalars * gate
        scored = silu * attn_ref[...]
        logits = [
            jnp.sum(scored[h * 16 : (h + 1) * 16], axis=0, keepdims=True)
            for h in range(HEADS)
        ]
        attention = jax.nn.sigmoid(jnp.concatenate(logits, axis=0))
        rot[0:CH, :] = silu.astype(BF16)

        @pl.loop(1, KEPT)
        def _(i):
            part_rows = pl.ds(pl.multiple_of(i * CH, CH), CH)
            rot[part_rows, :] = (hid[part_rows, :] * gate).astype(BF16)

        conv(1)
        grid[0:HEADS, :] = attention

        @pl.loop(0, HEADS)
        def _(c):
            base = c * 16
            weight = grid[pl.ds(c, 1), :]
            for degree in range(5):
                width = 2 * degree + 1
                rows = rows_of_degree(degree)
                inputs = [
                    hid[pl.ds(pl.multiple_of(place * CH + base, 16), 16), :] * weight
                    for place, _ in rows
                ]
                for j in range(width):
                    total = None
                    for value, (_, offset) in zip(inputs, rows):
                        k = weight_row(degree, offset, j)
                        term = packed_ref[k : k + 1, lanes] * value
                        total = term if total is None else total + term
                    msg[
                        pl.ds(pl.multiple_of((degree * degree + j) * CH + base, 16), 16), :
                    ] = total.astype(BF16)

        landing = (
            lax.broadcasted_iota(jnp.int32, (acc.shape[0], TILE), 0) == target
        ).astype(BF16)

        @pl.loop(0, 5)
        def _(part):
            at_part = pl.multiple_of(part * 5 * CH, 5 * CH)
            acc[:, pl.ds(at_part, 5 * CH)] += lax.dot_general(
                landing, msg[pl.ds(at_part, 5 * CH), :],
                (((1,), (1,)), ((), ())), preferred_element_type=F32,
            )
        return carry

    lax.fori_loop(0, pl.cdiv(total_ref[0], TILE), tile, 0)
    out_ref[...] = acc[...].astype(out_ref.dtype)


def edge_pass(atoms, total, packed, aux, attn, pieces, weights, acc, last):
    sizes = tuple(piece.shape[0] for piece in pieces)
    padded = -(-sum(sizes) // 128) * 128
    features = pieces[0].shape[1]
    anywhere = pl.BlockSpec(memory_space=pl.ANY)
    vmem = pl.BlockSpec(memory_space=VMEM)
    operands = [total, packed, aux, attn, *pieces, *weights]
    specs = [pl.BlockSpec(memory_space=pltpu.SMEM), vmem, vmem, vmem]
    specs += [anywhere] * (len(pieces) + 3)
    if acc is not None:
        operands.append(acc)
        specs.append(anywhere)
    return pl.pallas_call(
        functools.partial(edge_kernel, sizes, acc is not None, last),
        out_shape=jax.ShapeDtypeStruct((atoms, features), BF16 if last else F32),
        in_specs=specs,
        out_specs=vmem,
        scratch_shapes=[
            VMEM((padded, features), BF16),
            VMEM((features, padded), BF16),
            VMEM((features, TILE), F32),
            VMEM((KEPT * CH, TILE), BF16),
            VMEM((KEPT * CH, TILE), F32),
            VMEM((features, TILE), BF16),
            VMEM((atoms, features), F32),
            *[VMEM(w.shape, BF16) for w in weights],
            pltpu.SemaphoreType.DMA((len(pieces),)),
            pltpu.SemaphoreType.DMA((4,)),
        ],
        name="edges_last" if last else "edges_first",
    )(*operands)


def shift_pairs(count, step):
    return [((i + step) % count, i) for i in range(count)]


def exchange(block):
    n_x, n_y, n_z = (lax.axis_size(name) for name in ("gx", "gy", "gz"))
    partner_out = [(i, (i + 1) if i % 2 else (i - 1) % n_y) for i in range(n_y)]
    partner_out = [(i, j % n_y) for i, j in partner_out]
    partner_in = [(i, i ^ 1) for i in range(n_y)]
    y_steps = (1,) if n_x == 2 else (1, -1)
    z_steps = (1,) if n_z == 2 else (1, -1)
    pieces = {(0, 0, 0): block}

    def over_z(value, step):
        return lax.ppermute(value, "gz", shift_pairs(n_z, step))

    def over_y(value, step):
        return lax.ppermute(value, "gx", shift_pairs(n_x, step))

    def over_out(value):
        return lax.ppermute(value, "gy", partner_out)

    def over_both(value, step):
        pairs = [
            (s * n_y + i, d * n_y + j)
            for s, d in shift_pairs(n_x, step)
            for i, j in partner_out
        ]
        return lax.ppermute(value, ("gx", "gy"), pairs)

    for z in z_steps:
        pieces[z, 0, 0] = over_z(block, z)
    for y in y_steps:
        pieces[0, y, 1] = over_both(block, y)
    pieces[0, 0, 1] = over_out(block)
    for y in y_steps:
        pieces[0, y, 0] = over_y(block, y)
    for z in z_steps:
        for y in y_steps:
            pieces[z, y, 1] = over_z(pieces[0, y, 1], z)
            pieces[z, y, 0] = over_y(pieces[z, 0, 0], y)
        pieces[z, 0, 1] = over_out(pieces[z, 0, 0])
    for z in (0, *z_steps):
        for y in (0, *y_steps):
            pieces[z, y, 2] = lax.ppermute(pieces[z, y, 0], "gy", partner_in)
    return pieces


def is_late(key):
    z, y, x = key
    return z != 0 and (y != 0 or x == 1)


def tables(order, atoms, rows_each, n_x, n_z):
    luts = []
    for odd in (0, 1):
        base, which = [], []
        for da in (-1, 0, 1):
            for db in (-1, 0, 1):
                for dk in (-1, 0, 1):
                    z = abs(dk) if n_z == 2 else dk
                    y = abs(da) if n_x == 2 else da
                    inner = -1 if odd else 1
                    x = 0 if db == 0 else (2 if db == inner else 1)
                    late = int(is_late((z, y, x)))
                    offset = 0 if late else atoms
                    base.append(offset + rows_each * order[late].index((z, y, x)))
                    which.append(late)
        luts.append((tuple(base), tuple(which)))
    (even, pass_even), (odd_lut, pass_odd) = luts
    return atoms, rows_each, 2, even, odd_lut, pass_even, pass_odd


def body(
    coeffs, halo_rows, edge_source, edge_target, edge_count, block_count, wigner,
    w_zero, w_one, w_two, attn_vector,
):
    atoms, features = coeffs.shape[3:]
    blocks, size = edge_source.shape[3:]
    rows_each = halo_rows.shape[3]
    own = coeffs.reshape(atoms, features)
    block = boundary_rows(own, halo_rows.reshape(1, rows_each))
    pieces = exchange(block)
    order = (
        [key for key in pieces if not is_late(key)],
        [key for key in pieces if is_late(key)],
    )
    luts = tables(order, atoms, rows_each, lax.axis_size("gx"), lax.axis_size("gz"))
    scalars = jnp.stack([block_count.reshape(()), lax.axis_index("gy") % 2])
    normed, packed_a, aux_a, total_a, packed_b, aux_b, total_b = prepare(
        luts, scalars, edge_count.reshape(blocks), edge_source.reshape(blocks, size),
        edge_target.reshape(blocks, size), wigner.reshape(blocks, PACKED, size), own,
    )
    weights = [jnp.swapaxes(w, -1, -2) for w in (w_zero, w_one, w_two)]
    attn = jnp.broadcast_to(attn_vector[:, None], (CH, TILE))
    first = [normed] + [pieces[key] for key in order[0]]
    second = [pieces[key] for key in order[1]]
    partial = edge_pass(atoms, total_a, packed_a, aux_a, attn, first, weights, None, False)
    update = edge_pass(atoms, total_b, packed_b, aux_b, attn, second, weights, partial, True)
    return update.reshape(1, 1, 1, atoms, features)


def solution(mesh):
    placed = (
        P("gx", "gy", "gz", None, None),
        P("gx", "gy", "gz", None),
        P("gx", "gy", "gz", None, None),
        P("gx", "gy", "gz", None, None),
        P("gx", "gy", "gz", None),
        P("gx", "gy", "gz"),
        P("gx", "gy", "gz", None, None, None),
        P(),
        P(),
        P(),
        P(),
    )
    return jax.shard_map(
        body, mesh=mesh, in_specs=placed, out_specs=P("gx", "gy", "gz", None, None),
        check_vma=False,
    )
```
